32 devices in a mesh: ctx: 8 (over y, x, core), fsdp: 4 (over z).
Axes of the slice: x: 2, y: 2, z: 4, core: 2. Of those that a mesh axis runs over, the one named last changes fastest.
Arguments:
- xbc: bfloat16 [4, 1024, 9216], P('fsdp', 'ctx'), may hold values from -6 to 6
- dt_raw: bfloat16 [4, 128, 1024], P('fsdp', None, 'ctx'), may hold values from -4 to 15
- dy: bfloat16 [4, 1024, 8192], P('fsdp', 'ctx'), may hold values from -6 to 6
- conv_params: float32 [5, 9216], replicated, may hold values from -3 to 3
- head_params: float32 [3, 128], replicated, may hold values from -13 to 1.5, as said below
Outputs:
- d_xbc: bfloat16 [4, 1024, 9216], P('fsdp', 'ctx')
- d_dt_raw: float32 [4, 128, 1024], P('fsdp', None, 'ctx')
- d_conv: float32 [5, 9216], replicated
- d_head: float32 [3, 128], replicated
The draws below stay inside these ranges and needn't reach their ends.
Inputs may be any that keep to these rules, and one draw needn't show every extreme that they name: `head_params`: head parameters.
All inputs are finite; a program needn't handle non-finite values.
Results may differ from the reference program's by a relative error of at most 0.007.
Values may be sent and summed in bfloat16 or wider, within the bound.
A program may use at most 256 MiB of HBM per device.

```python
import jax
import jax.numpy as jnp
from jax import lax

HEADS = 128
HEAD_DIM = 64
STATE = 128
GROUPS = 4
CONV_W = 4
SPAN = 128
TOK_DEV = 128
SEQ_LEN = 1024
BATCH = 4
CHANNELS = 9216


def draw_head_params(key, part):
    keys = jax.random.split(jax.random.fold_in(key, 11), 5)
    share = 0.5
    fast_heads = jax.random.bernoulli(keys[0], share, (HEADS,))
    slow_level = jax.random.uniform(keys[1], (HEADS,), jnp.float32, 0.15, 0.4)
    slow_bias = jnp.log(slow_level / (SEQ_LEN * 1.0))
    fast_bias = jax.random.uniform(keys[2], (HEADS,), jnp.float32, -2.6, -1.9)
    spread_log = jax.random.uniform(keys[3], (HEADS,), jnp.float32, -0.5, 0.5)
    log_rate = jnp.where(fast_heads, jnp.log(0.25) + spread_log, spread_log)
    step_bias = jnp.where(fast_heads, fast_bias, slow_bias)
    skip_gain = jax.random.uniform(keys[4], (HEADS,), jnp.float32, 0.5, 1.5)
    return jnp.stack([step_bias, log_rate, skip_gain]).astype(jnp.float32)


def draw_dt_raw(key, part):
    keys = jax.random.split(jax.random.fold_in(key, 23), 4)
    shape_full = (BATCH, HEADS, SEQ_LEN)
    stochastic_perturbation = jnp.clip(0.8 * jax.random.normal(keys[0], shape_full, jnp.float32), -3.2, 3.2)
    segment = TOK_DEV // 2
    segment_count = SEQ_LEN // segment
    beginning_displacements = jax.random.uniform(keys[1], (BATCH, 1, segment_count), jnp.float32, -0.8, 0.8)
    beginning_displacements = jnp.repeat(beginning_displacements, segment, axis=2)
    drawn_locations = jax.random.randint(keys[2], (BATCH, 3), 0, SEQ_LEN)
    tier_magnitudes = jnp.log(SEQ_LEN * 1.0) + jax.random.uniform(keys[3], (BATCH, 3), jnp.float32, 0.0, 0.5)
    segment_positions = jnp.arange(SEQ_LEN)
    cluster_sets = jnp.sum(jnp.where(segment_positions[None, None, :] == drawn_locations[:, :, None], tier_magnitudes[:, :, None], 0.0), axis=1)
    overall_accumulation = jnp.clip(stochastic_perturbation + beginning_displacements + cluster_sets[:, None, :], -4.0, 15.0)
    return overall_accumulation.astype(jnp.bfloat16)


def level_of(stream_key, shape, cuts, least, top_value):
    factor_of, own = 1.0, jax.random.fold_in(stream_key, 6)
    for dim, parts in cuts:
        steps = jnp.exp(jax.random.uniform(jax.random.fold_in(own, dim), (parts,), jnp.float32, least / len(cuts), top_value / len(cuts)))
        factor_of = factor_of * jnp.repeat(steps, shape[dim] // parts).reshape([-1 if axis == dim else 1 for axis in range(len(shape))])
    return factor_of


def scatter_about(stream_key, dims, width, limit, cuts=(), kind=jnp.bfloat16):
    result = width * jax.random.normal(stream_key, dims, jnp.float32)
    if cuts:
        result = result * level_of(stream_key, dims, cuts, -0.22, 0.18)
    return jnp.clip(result, -limit, limit).astype(kind)


def setup_inputs(seed: int = 0) -> dict:
    arg_keys = jax.random.split(jax.random.key(seed), 6)
    xbc = scatter_about(arg_keys[0], (BATCH, SEQ_LEN, CHANNELS), 1.0, 6.0, ((0, 4), (1, 8)))
    dt_raw = draw_dt_raw(jax.random.fold_in(arg_keys[5], 71), 0)
    dy = scatter_about(arg_keys[2], (BATCH, SEQ_LEN, HEADS * HEAD_DIM), 1.0, 6.0, ((0, 4), (1, 8)))
    conv_params = scatter_about(arg_keys[3], (CONV_W + 1, CHANNELS), 0.5, 3.0, (), jnp.float32)
    head_params = draw_head_params(jax.random.fold_in(arg_keys[5], 71), 0)
    return dict(xbc=xbc, dt_raw=dt_raw, dy=dy, conv_params=conv_params, head_params=head_params)


exact_prec = lax.Precision.HIGHEST

def split_channels(activated):
    row_count = activated.shape[0]
    x_width = HEADS * HEAD_DIM
    bc_width = GROUPS * STATE
    x_heads = activated[:, :x_width].reshape(row_count, HEADS, HEAD_DIM)
    b_groups = activated[:, x_width:x_width + bc_width].reshape(row_count, GROUPS, STATE)
    c_groups = activated[:, x_width + bc_width:].reshape(row_count, GROUPS, STATE)
    return (x_heads, b_groups, c_groups)

def prepare(extended, dt_values, conv_params, head_params):
    row_count = extended.shape[0] - (CONV_W - 1)
    mixed_in = jnp.broadcast_to(conv_params[CONV_W][None, :], (row_count, extended.shape[1]))
    for offset in range(CONV_W):
        mixed_in = mixed_in + conv_params[offset][None, :] * extended[offset:offset + row_count]
    activated = jax.nn.silu(mixed_in)
    x_heads, b_groups, c_groups = split_channels(activated)
    step_size = jax.nn.softplus(dt_values + head_params[0][:, None])
    rates = step_size * jnp.exp(head_params[1])[:, None]
    return (x_heads, b_groups, c_groups, step_size, rates)

def span_outputs(x_heads, b_groups, c_groups, step_size, rates, head_params):
    row_count = x_heads.shape[0]
    block_count = row_count // SPAN
    per_group = HEADS // GROUPS
    x_blocks = x_heads.reshape(block_count, SPAN, HEADS, HEAD_DIM)
    b_blocks = b_groups.reshape(block_count, SPAN, GROUPS, STATE)
    c_blocks = c_groups.reshape(block_count, SPAN, GROUPS, STATE)
    d_blocks = step_size.reshape(HEADS, block_count, SPAN).transpose(1, 0, 2)
    l_blocks = rates.reshape(HEADS, block_count, SPAN).transpose(1, 0, 2)
    causal_mask = jnp.arange(SPAN)[:, None] >= jnp.arange(SPAN)[None, :]

    def advance(state_now, block):
        x_block, b_block, c_block, d_block, l_block = block
        running = jnp.cumsum(l_block, axis=1)
        spacing = jnp.where(causal_mask[None], running[:, :, None] - running[:, None, :], 0.0)
        fading = jnp.where(causal_mask[None], jnp.exp(-spacing), 0.0)
        scores = jnp.einsum('tgn,sgn->gts', c_block, b_block, precision=exact_prec)
        weights = scores[:, None] * fading.reshape(GROUPS, per_group, SPAN, SPAN) * d_block.reshape(GROUPS, per_group, 1, SPAN)
        x_grouped = x_block.reshape(SPAN, GROUPS, per_group, HEAD_DIM)
        outputs = jnp.einsum('gkts,sgkp->tgkp', weights, x_grouped, precision=exact_prec)
        carried = jnp.einsum('tgn,gkpn->tgkp', c_block, state_now.reshape(GROUPS, per_group, HEAD_DIM, STATE), precision=exact_prec)
        decay_rows = jnp.exp(-running).T.reshape(SPAN, GROUPS, per_group)[..., None]
        outputs = (outputs + carried * decay_rows).reshape(SPAN, HEADS, HEAD_DIM)
        tail_weight = (jnp.exp(running - running[:, -1:]) * d_block).T
        weighted = (tail_weight[:, :, None] * x_block).reshape(SPAN, GROUPS, per_group, HEAD_DIM)
        fresh_state = jnp.einsum('sgkp,sgn->gkpn', weighted, b_block, precision=exact_prec).reshape(HEADS, HEAD_DIM, STATE)
        state_next = jnp.exp(-running[:, -1])[:, None, None] * state_now + fresh_state
        return (state_next, outputs)
    initial = jnp.zeros((HEADS, HEAD_DIM, STATE), jnp.float32)
    _, outputs = lax.scan(advance, initial, (x_blocks, b_blocks, c_blocks, d_blocks, l_blocks))
    outputs = outputs.reshape(row_count, HEADS, HEAD_DIM) + head_params[2][None, :, None] * x_heads
    return outputs.reshape(row_count, HEADS * HEAD_DIM)

def sequence_grads(xbc_seq, dt_seq, dy_seq, conv_params, head_params):

    def forward(xbc_values, dt_values, conv_values, head_values):
        padding = jnp.zeros((CONV_W - 1, xbc_values.shape[1]), jnp.float32)
        extended = jnp.concatenate([padding, xbc_values], axis=0)
        pieces = prepare(extended, dt_values, conv_values, head_values)
        return span_outputs(*pieces, head_values)
    _, pullback = jax.vjp(forward, xbc_seq.astype(jnp.float32), dt_seq.astype(jnp.float32), conv_params, head_params)
    return pullback(dy_seq.astype(jnp.float32))

def reference(xbc, dt_raw, dy, conv_params, head_params):

    def per_sequence(sample):
        return sequence_grads(sample[0], sample[1], sample[2], conv_params, head_params)
    grad_x, grad_dt, grad_conv, grad_head = lax.map(per_sequence, (xbc, dt_raw, dy))
    return (grad_x.astype(jnp.bfloat16), grad_dt, lax.optimization_barrier(jnp.sum(grad_conv, axis=0)), lax.optimization_barrier(jnp.sum(grad_head, axis=0)))
```

```python
import functools

import jax
import jax.numpy as jnp
from jax import lax
from jax.experimental import pallas as pl
from jax.experimental.pallas import tpu as pltpu
from jax.sharding import PartitionSpec as P

HEADS = 128
HEAD_DIM = 64
STATE = 128
GROUPS = 4
CONV_W = 4
T = 128
LANES = 128
X_WIDTH = HEADS * HEAD_DIM
CHANNELS = X_WIDTH + 2 * GROUPS * STATE
PAIRS = HEADS // 2
PER_GROUP = PAIRS // GROUPS
F32 = jnp.float32
BF16 = jnp.bfloat16
MESH = pl.DeviceIdType.MESH
CHUNKS = 32
CHUNK_HEADS = HEADS // CHUNKS
CHUNK_ROWS = X_WIDTH // CHUNKS
CHUNK_PAIRS = PAIRS // CHUNKS
GROUP_CHUNKS = CHUNKS // GROUPS
LAG_CORE = 1
LAG_CHIP = 3
TAIL = 16
RIM = 4
HALO_CUTS = (0, 16, 40, 72)
HALOS = len(HALO_CUTS) - 1
BLOCKS = CHANNELS // LANES
GROUP_BLOCKS = PER_GROUP + 2
LOG2E = 1.4426950408889634


def dot(a, b, ca, cb, precision=None):
    return lax.dot_general(
        a, b, (((ca,), (cb,)), ((), ())), precision=precision, preferred_element_type=F32
    )


def block_of(i):
    return pl.ds(pl.multiple_of(i * LANES, LANES), LANES)


def sigmoid(v):
    return 1.0 / (1.0 + jnp.exp(-v))


def softplus(v):
    z = jnp.exp(-jnp.abs(v))
    small = z * (1.0 - z * (0.5 - z * (1.0 / 3.0 - z * 0.25)))
    return jnp.maximum(v, 0.0) + jnp.where(z < 0.01, small, jnp.log(1.0 + z))


def iota2(shape, dim):
    return lax.broadcasted_iota(jnp.int32, shape, dim)


def wide_pair(ht_ref, h):
    top = jnp.broadcast_to(ht_ref[pl.ds(h, 1), :], (HEAD_DIM, T))
    low = jnp.broadcast_to(ht_ref[pl.ds(h + 1, 1), :], (HEAD_DIM, T))
    return jnp.concatenate([top, low], axis=0).T


def main_kernel(
    counts,
    xbc_ref, dt_ref, dy_ref, conv_ref, head_ref,
    dx_ref, ddt_ref, dconv_ref, dhead_ref,
    ext, dms, mixed_ref, xd_ref, y_ref, dxd_ref, leave_ref, pull_ref,
    out_f, out_b, in_f, in_b, stepw_ref, headw_ref, tailw_ref,
    fade_ref, run_ref, step_ref, skip_ref, b_ref, c_ref,
    scores, dscores, db, dc, acc, halo_out, halo_in, rim_out, rim_in, tail_ref,
    packed, parts, mine, planes, total,
    send_f, recv_f, send_b, recv_b, send_h, recv_h, send_r, recv_r,
    send_s, recv_s, send_z, recv_z, send_g, recv_g,
):
    count, depth = counts
    share = packed.shape[1] // count
    me, plane = lax.axis_index("ctx"), lax.axis_index("fsdp")
    first, last = me == 0, me == count - 1
    up = jnp.minimum(me + 1, count - 1)
    down = jnp.maximum(me - 1, 0)
    barrier = pltpu.get_barrier_semaphore()
    for r in range(1, count):
        peer = lax.rem(me + r, count)
        pl.semaphore_signal(barrier, inc=1, device_id={"ctx": peer}, device_id_type=MESH)
    for r in range(1, depth):
        peer = lax.rem(plane + r, depth)
        pl.semaphore_signal(barrier, inc=1, device_id={"fsdp": peer}, device_id_type=MESH)

    def remote(src, dst, send, recv, **to):
        return pltpu.make_async_remote_copy(
            src_ref=src, dst_ref=dst, send_sem=send, recv_sem=recv,
            device_id=to, device_id_type=MESH,
        )

    for i in range(BLOCKS):
        edge = xbc_ref[T - TAIL :, i * LANES : (i + 1) * LANES].astype(F32)
        halo_out[(i + BLOCKS - PAIRS) % BLOCKS] = edge[TAIL - RIM :, :]
    pl.semaphore_wait(barrier, count + depth - 2)

    def halo(k):
        rows = pl.ds(HALO_CUTS[k], HALO_CUTS[k + 1] - HALO_CUTS[k])
        return remote(halo_out.at[rows], halo_in.at[rows], send_h.at[k], recv_h.at[k], ctx=up)

    @pl.when(jnp.logical_not(last))
    def _():
        for k in range(HALOS):
            halo(k).start()

    step_th = softplus(dt_ref[...].astype(F32).T + head_ref[0:1, :])
    rate_th = step_th * (jnp.exp(head_ref[1:2, :]) * LOG2E)
    lower = (iota2((T, T), 0) >= iota2((T, T), 1)).astype(F32)
    run_ht = dot(lower, rate_th, 1, 0, lax.Precision.HIGHEST).T
    run_ref[...] = run_ht
    step_ref[...] = step_th.T
    fade_ref[...] = jnp.broadcast_to(jnp.exp2(-run_ht[:, T - 1 : T]), (HEADS, LANES))
    skip_ref[...] = jnp.broadcast_to(head_ref[2:3, :], (LANES, HEADS)).T
    acc[...] = jnp.zeros_like(acc)
    packed[...] = jnp.zeros_like(packed)
    dscores[...] = jnp.zeros_like(dscores)
    for slot in range(2):
        dms[slot, 0:8, :] = jnp.zeros((8, LANES), F32)
        dms[slot, 8 + T : 16 + T, :] = jnp.zeros((8, LANES), F32)
    causal = iota2((T, T), 0) >= iota2((T, T), 1)
    left = iota2((T, LANES), 1) < HEAD_DIM
    zero = jnp.zeros((T, LANES), BF16)

    @pl.when(first)
    def _():
        halo_in[...] = jnp.zeros_like(halo_in)

    @pl.when(jnp.logical_not(first))
    def _():
        halo(0).wait_recv()

    def split(v):
        return jnp.concatenate([jnp.where(left, v, zero), jnp.where(left, zero, v)], 0)

    def convolve(i):
        cols = block_of(i)
        ext[i, RIM : 8, :] = halo_in[lax.rem(i + BLOCKS - PAIRS, BLOCKS)]
        ext[i, 8 : 8 + T, :] = xbc_ref[:, cols].astype(F32)
        mixed = conv_ref[CONV_W : CONV_W + 1, cols] + conv_ref[0:1, cols] * ext[i, 5 : 5 + T, :]
        for j in range(1, CONV_W):
            mixed = mixed + conv_ref[j : j + 1, cols] * ext[i, 5 + j : 5 + j + T, :]
        mixed_ref[:, cols] = mixed
        return mixed * sigmoid(mixed)

    def bc(g, _):
        b16 = convolve(PAIRS + g).astype(BF16)
        c16 = convolve(PAIRS + GROUPS + g).astype(BF16)
        b_ref[:, block_of(g)] = b16
        c_ref[:, block_of(g)] = c16
        scores[g] = dot(c16, b16, 1, 1)
        return 0

    lax.fori_loop(0, GROUPS, bc, 0)

    def front(i):
        h = 2 * i
        g = i // PER_GROUP
        cols = block_of(i)
        x = convolve(i)
        row = [jnp.broadcast_to(run_ref[pl.ds(h + k, 1), :], (T, T)) for k in range(2)]
        col = [r.T for r in row]
        run = jnp.where(left, col[0], col[1])
        step = wide_pair(step_ref, h)
        xd = (x * step).astype(BF16)
        e_tail = jnp.exp2(run - run[T - 1 : T, :])
        e_head = jnp.exp2(-run)
        stepw_ref[:, cols] = step
        headw_ref[:, cols] = e_head
        tailw_ref[:, cols] = e_tail
        xd_ref[:, cols] = xd
        dy16 = dy_ref[:, cols]
        tail = (xd.astype(F32) * e_tail).astype(BF16)
        out = (e_head * dy16.astype(F32)).astype(BF16)
        leave_ref[cols, :] = dot(tail, b_ref[:, block_of(g)], 0, 0)
        pull_ref[cols, :] = dot(out, c_ref[:, block_of(g)], 0, 0)
        fades = [jnp.exp2(jnp.where(causal, row[k] - col[k], -1e30)) for k in range(2)]
        bd_x = split(xd)
        sc = scores[g]
        w = [(sc * f).astype(BF16) for f in fades]
        y_ref[:, cols] = dot(jnp.concatenate(w, 1), bd_x, 1, 0)
        dxd_ref[:, cols] = dot(jnp.concatenate(w, 0), split(dy16), 0, 0)
        pairwise = dot(dy16, bd_x, 1, 1)
        dscores[g] += pairwise[:, :T] * fades[0] + pairwise[:, T:] * fades[1]

    def rows_of(c):
        return pl.ds(pl.multiple_of(c * CHUNK_ROWS, CHUNK_ROWS), CHUNK_ROWS)

    def copy(c, src, dst, send, recv, peer):
        return remote(src.at[rows_of(c)], dst.at[rows_of(c)], send.at[c], recv.at[c], ctx=peer)

    def handle(c, own, src, dst, send, recv, peer, begins, ends):
        @pl.when(begins)
        def _():
            dst[rows_of(c), :] = jnp.zeros((CHUNK_ROWS, LANES), BF16)

        @pl.when(jnp.logical_not(begins))
        def _():
            copy(c, src, dst, send, recv, peer).wait_recv()

        @pl.when(jnp.logical_not(ends))
        def _():
            for k in range(CHUNK_HEADS):
                rows = pl.ds(pl.multiple_of(c * CHUNK_ROWS + k * HEAD_DIM, HEAD_DIM), HEAD_DIM)
                fade = fade_ref[pl.ds(c * CHUNK_HEADS + k, 1), :]
                src[rows, :] = (fade * dst[rows, :].astype(F32) + own[rows, :]).astype(BF16)
            copy(c, src, dst, send, recv, peer).start()

    def conv_back(i, at, slot, mixed, sig, dact):
        g, k = at
        cols = block_of(i)
        dm = dact * (sig * (1.0 + mixed * (1.0 - sig)))
        dms[slot, 8 : 8 + T, :] = dm
        taps = [conv_ref[j : j + 1, cols] for j in range(CONV_W)]
        own = taps[3] * dm
        rim = taps[0] * dms[slot, 8:16, :]
        for j in range(3):
            own = own + taps[j] * dms[slot, 11 - j : 11 - j + T, :]
        for j in range(1, 3):
            rim = rim + taps[j] * dms[slot, 8 - j : 16 - j, :]
        dx_ref[:, cols] = own.astype(BF16)
        tail_ref[i] = own[T - TAIL :, :]
        rim_out[g, k] = rim[0:RIM, :]
        for j in range(CONV_W):
            packed[g, k, j : j + 1, :] = jnp.sum(dm * ext[i, 5 + j : 5 + j + T, :], 0, keepdims=True)
        packed[g, k, CONV_W : CONV_W + 1, :] = jnp.sum(dm, 0, keepdims=True)

    def pair(i, slot):
        h = 2 * i
        g = i // PER_GROUP
        cols = block_of(i)
        mixed = mixed_ref[:, cols]
        sig = sigmoid(mixed)
        x = mixed * sig
        dy = dy_ref[:, cols].astype(F32)
        step = stepw_ref[:, cols]
        xd = xd_ref[:, cols].astype(F32)
        e_tail = tailw_ref[:, cols]
        e_head = headw_ref[:, cols]
        enter = in_f[cols, :]
        later = in_b[cols, :]
        y = y_ref[:, cols] + e_head * dot(c_ref[:, block_of(g)], enter, 1, 1)
        from_tail = e_tail * dot(b_ref[:, block_of(g)], later, 1, 1)
        dxd = dxd_ref[:, cols] + from_tail
        dc[...] += dot((e_head * dy).astype(BF16), enter, 1, 0)
        db[...] += dot((xd * e_tail).astype(BF16), later, 1, 0)
        skip = jnp.where(left[0:1, :], skip_ref[pl.ds(h, 1), :], skip_ref[pl.ds(h + 1, 1), :])
        conv_back(i, (g, lax.rem(i, PER_GROUP)), slot, mixed, sig, step * dxd + skip * dy)
        both = (enter.astype(F32) * later.astype(F32)).astype(BF16)
        passed = dot(jnp.ones((8, STATE), BF16), both, 1, 1)
        sub = iota2((8, LANES), 0)
        rows = jnp.where(sub == 0, jnp.sum(dy * x, 0, keepdims=True), 0.0)
        rows = rows + jnp.where(
            sub == 1,
            jnp.sum(xd * from_tail, 0, keepdims=True) + e_head[T - 1 : T, :] * passed[0:1, :],
            0.0,
        )
        value = jnp.concatenate([xd * dxd - dy * y, x * dxd, rows], 0)
        high = value.astype(BF16)
        low = (value - high.astype(F32)).astype(BF16)
        pick = (iota2((LANES, HEADS), 1) == h + iota2((LANES, HEADS), 0) // HEAD_DIM).astype(BF16)
        acc[...] += dot(
            jnp.concatenate([high, low], 1), jnp.concatenate([pick, pick], 0), 1, 0
        )

    def piece(k):
        return pl.ds(k * share, share)

    def rim_copy(g):
        return remote(rim_out.at[g], rim_in.at[g], send_r.at[g], recv_r.at[g], ctx=down)

    def scatter(g, peer, slot):
        return remote(
            packed.at[g, piece(peer)], parts.at[g, slot],
            send_s.at[g, peer], recv_s.at[g, slot], ctx=peer,
        )

    def across(g, peer, slot):
        return remote(
            mine.at[g], planes.at[g, slot], send_z.at[g, peer], recv_z.at[g, slot], fsdp=peer
        )

    def gather(g, peer, slot):
        return remote(
            total.at[g, piece(me)], total.at[g, piece(slot)],
            send_g.at[g, peer], recv_g.at[g, slot], ctx=peer,
        )

    def share_out(g):
        for r in range(1, count):
            scatter(g, lax.rem(me + r, count), me).start()
        parts[g, me] = packed[g, piece(me)]

    def sum_ctx(g):
        for r in range(1, count):
            scatter(g, me, lax.rem(me + r, count)).wait_recv()
        own = parts[g, 0]
        for k in range(1, count):
            own = own + parts[g, k]
        mine[g] = own
        for r in range(1, depth):
            across(g, lax.rem(plane + r, depth), plane).start()
        planes[g, plane] = own

    def sum_fsdp(g):
        for r in range(1, depth):
            across(g, plane, lax.rem(plane + r, depth)).wait_recv()
        own = planes[g, 0]
        for k in range(1, depth):
            own = own + planes[g, k]
        total[g, piece(me)] = own
        for r in range(1, count):
            gather(g, lax.rem(me + r, count), me).start()

    def place(g, k):
        return jnp.where(k < PER_GROUP, g * PER_GROUP + k, PAIRS + g + (k - PER_GROUP) * GROUPS)

    def finish(g):
        for r in range(1, count):
            gather(g, me, lax.rem(me + r, count)).wait_recv()

        def spread(k, _):
            dconv_ref[:, block_of(place(g, k))] = total[g, k, 0 : CONV_W + 1, :]
            return 0

        lax.fori_loop(0, GROUP_BLOCKS, spread, 0)

    def seam(g):
        @pl.when(jnp.logical_not(last))
        def _():
            rim_copy(g).wait_recv()

            def fix(k, _):
                i = place(g, k)
                pad = jnp.zeros((TAIL - (CONV_W - 1), LANES), F32)
                moved = jnp.concatenate([pad, rim_in[g, k][0 : CONV_W - 1, :]], 0)
                dx_ref[T - TAIL :, block_of(i)] = (tail_ref[i] + moved).astype(BF16)
                return 0

            lax.fori_loop(0, GROUP_BLOCKS, fix, 0)

    def close_group(g):
        ds = dscores[g].astype(BF16)
        b16 = b_ref[:, block_of(g)]
        c16 = c_ref[:, block_of(g)]
        for slot, k, at, sums in (
            (0, PER_GROUP, PAIRS + g, db[...] + dot(ds, c16, 0, 0)),
            (1, PER_GROUP + 1, PAIRS + GROUPS + g, dc[...] + dot(ds, b16, 1, 0)),
        ):
            mixed = mixed_ref[:, block_of(at)]
            conv_back(at, (g, k), slot, mixed, sigmoid(mixed), sums)

        @pl.when(jnp.logical_not(first))
        def _():
            rim_copy(g).start()

    def lag(place):
        return (place + 1) // 2 * LAG_CORE + place // 2 * LAG_CHIP

    lag_f, lag_b = lag(me), lag(count - 1 - me)
    delay = jnp.maximum(lag_f, lag_b)
    longest = lag(count - 1)

    def phase(v, wait, act, most=GROUPS - 1):
        q = v - (longest + GROUP_CHUNKS - 1 + wait)
        g = q // GROUP_CHUNKS

        @pl.when(jnp.logical_and(q >= 0, jnp.logical_and(lax.rem(q, GROUP_CHUNKS) == 0, g < most)))
        def _():
            act(g)

    def fronts(c):
        for k in range(CHUNK_PAIRS):
            front(c * CHUNK_PAIRS + k)

    fronts(0)

    def tick(v, _):
        c = v - lag_f

        for q in range(1, HALOS):
            @pl.when(jnp.logical_and(v == (HALO_CUTS[q] + PAIRS - BLOCKS) // CHUNK_PAIRS - 1, jnp.logical_not(first)))
            def _():
                halo(q).wait_recv()

        @pl.when(jnp.logical_and(c >= 0, c < CHUNKS))
        def _():
            handle(c, leave_ref, out_f, in_f, send_f, recv_f, up, first, last)

        d = v - lag_b

        @pl.when(jnp.logical_and(d >= 0, d < CHUNKS))
        def _():
            handle(d, pull_ref, out_b, in_b, send_b, recv_b, down, last, first)

        @pl.when(v + 1 < CHUNKS)
        def _():
            fronts(v + 1)

        w = v - delay
        inside = jnp.logical_and(w >= 0, w < CHUNKS)

        @pl.when(jnp.logical_and(inside, lax.rem(w, GROUP_CHUNKS) == 0))
        def _():
            db[...] = jnp.zeros_like(db)
            dc[...] = jnp.zeros_like(dc)

        @pl.when(inside)
        def _():
            for k in range(CHUNK_PAIRS):
                pair(w * CHUNK_PAIRS + k, k)

        @pl.when(jnp.logical_and(inside, lax.rem(w, GROUP_CHUNKS) == GROUP_CHUNKS - 1))
        def _():
            g = w // GROUP_CHUNKS
            close_group(g)

            @pl.when(g < GROUPS - 1)
            def _():
                share_out(g)

        phase(v, 4, sum_ctx)
        phase(v, 5, seam)
        phase(v, 8, sum_fsdp, GROUPS - 2)
        return 0

    lax.fori_loop(0, CHUNKS + longest, tick, 0)

    upper = (iota2((T, T), 0) <= iota2((T, T), 1)).astype(F32)
    d_rate = dot(upper, acc[0:T, :], 1, 0, lax.Precision.HIGHEST) - acc[2 * T + 1 : 2 * T + 2, :]
    scale = jnp.exp(head_ref[1:2, :])
    raw = dt_ref[...].astype(F32).T + head_ref[0:1, :]
    d_dt = (acc[T : 2 * T, :] + d_rate * scale) * sigmoid(raw)
    end = GROUPS - 1
    packed[end, GROUP_BLOCKS, 0:1, :] = jnp.sum(d_dt, 0, keepdims=True)
    packed[end, GROUP_BLOCKS, 1:2, :] = jnp.sum(d_rate * softplus(raw) * scale, 0, keepdims=True)
    packed[end, GROUP_BLOCKS, 2:3, :] = acc[2 * T : 2 * T + 1, :]
    share_out(end)
    ddt_ref[...] = d_dt.T
    sum_ctx(end)
    sum_fsdp(end - 1)
    seam(end)

    def drain(c, _):
        @pl.when(jnp.logical_not(last))
        def _():
            copy(c, out_f, in_f, send_f, recv_f, up).wait_send()

        @pl.when(jnp.logical_not(first))
        def _():
            copy(c, out_b, in_b, send_b, recv_b, down).wait_send()

        return 0

    lax.fori_loop(0, CHUNKS, drain, 0)

    @pl.when(jnp.logical_not(last))
    def _():
        for k in range(HALOS):
            halo(k).wait_send()

    def settle(g, _):
        for r in range(1, count):
            scatter(g, lax.rem(me + r, count), me).wait_send()
        for r in range(1, depth):
            across(g, lax.rem(plane + r, depth), plane).wait_send()

        @pl.when(jnp.logical_not(first))
        def _():
            rim_copy(g).wait_send()

        return 0

    lax.fori_loop(0, GROUPS, settle, 0)
    sum_fsdp(end)
    for g in range(GROUPS):
        finish(g)
    dhead_ref[...] = total[end, GROUP_BLOCKS, 0:3, :]

    def settle_last(g, _):
        for r in range(1, count):
            gather(g, lax.rem(me + r, count), me).wait_send()
        return 0

    lax.fori_loop(0, GROUPS, settle_last, 0)


def vmem(count):
    return [pl.BlockSpec(memory_space=pltpu.VMEM)] * count


def call(kernel, out, scratch, args, limit=56, **params):
    return pl.pallas_call(
        kernel,
        out_shape=[jax.ShapeDtypeStruct(s, d) for s, d in out],
        in_specs=vmem(len(args)),
        out_specs=vmem(len(out)),
        scratch_shapes=scratch,
        compiler_params=pltpu.CompilerParams(vmem_limit_bytes=limit << 20, **params),
    )(*args)


def shards(xbc, dt_raw, dy, conv_params, head_params):
    count, depth = lax.axis_size("ctx"), lax.axis_size("fsdp")
    share = pl.cdiv(GROUP_BLOCKS + 1, count)
    wide, wide16 = pltpu.VMEM((T, X_WIDTH), F32), pltpu.VMEM((T, X_WIDTH), BF16)
    tall, tall16 = pltpu.VMEM((X_WIDTH, STATE), F32), pltpu.VMEM((X_WIDTH, STATE), BF16)
    small = pltpu.VMEM((T, LANES), F32)
    narrow = pltpu.VMEM((T, GROUPS * STATE), BF16)
    square = pltpu.VMEM((GROUPS, T, T), F32)
    edge = pltpu.VMEM((BLOCKS, RIM, LANES), F32)
    rim = pltpu.VMEM((GROUPS, GROUP_BLOCKS, RIM, LANES), F32)
    whole = pltpu.VMEM((GROUPS, share * count, 8, LANES), F32)
    dma = pltpu.SemaphoreType.DMA
    dx, ddt, dconv, dhead = call(
        functools.partial(main_kernel, (count, depth)),
        [((T, CHANNELS), BF16), ((HEADS, T), F32), ((CONV_W + 1, CHANNELS), F32), ((3, HEADS), F32)],
        [pltpu.VMEM((BLOCKS, 8 + T, LANES), F32), pltpu.VMEM((2, 16 + T, LANES), F32),
         pltpu.VMEM((T, CHANNELS), F32), wide16, wide, wide, tall, tall,
         tall16, tall16, tall16, tall16, wide, wide, wide,
         small, small, small, small, narrow, narrow,
         square, square, small, small, pltpu.VMEM((2 * T + 8, HEADS), F32),
         edge, edge, rim, rim, pltpu.VMEM((BLOCKS, TAIL, LANES), F32),
         whole, pltpu.VMEM((GROUPS, count, share, 8, LANES), F32),
         pltpu.VMEM((GROUPS, share, 8, LANES), F32),
         pltpu.VMEM((GROUPS, depth, share, 8, LANES), F32), whole]
        + [dma((CHUNKS,))] * 4 + [dma((HALOS,))] * 2 + [dma((GROUPS,))] * 2
        + [dma((GROUPS, count))] * 2 + [dma((GROUPS, depth))] * 2 + [dma((GROUPS, count))] * 2,
        (xbc[0], dt_raw[0], dy[0], conv_params, head_params),
        limit=63,
        collective_id=0,
        has_side_effects=True,
    )
    return dx[None], ddt[None], dconv, dhead


def solution(mesh):
    return jax.shard_map(
        shards,
        mesh=mesh,
        in_specs=(P("fsdp", "ctx", None), P("fsdp", None, "ctx"), P("fsdp", "ctx", None), P(), P()),
        out_specs=(P("fsdp", "ctx", None), P("fsdp", None, "ctx"), P(), P()),
        check_vma=False,
    )
```

```python
import functools

import jax
import jax.numpy as jnp
from jax import lax
from jax.experimental import pallas as pl
from jax.experimental.pallas import tpu as pltpu
from jax.sharding import PartitionSpec as P

HEADS = 128
HEAD_DIM = 64
STATE = 128
GROUPS = 4
CONV_W = 4
T = 128
LANES = 128
X_WIDTH = HEADS * HEAD_DIM
CHANNELS = X_WIDTH + 2 * GROUPS * STATE
PAIRS = HEADS // 2
PER_GROUP = PAIRS // GROUPS
F32 = jnp.float32
BF16 = jnp.bfloat16
MESH = pl.DeviceIdType.MESH
CHUNKS = 32
CHUNK_HEADS = HEADS // CHUNKS
CHUNK_ROWS = X_WIDTH // CHUNKS
CHUNK_PAIRS = PAIRS // CHUNKS
GROUP_CHUNKS = CHUNKS // GROUPS
LAG_CORE = 2
LAG_CHIP = 4
LAG_CROSS = 7
LAG_RELAY = 3
TAIL = 16
LANDINGS = 8
RIM = 4
HALO_CUTS = (0, 16, 40, 72)
HALOS = len(HALO_CUTS) - 1
BLOCKS = CHANNELS // LANES
GROUP_BLOCKS = PER_GROUP + 2
LOG2E = 1.4426950408889634


def dot(a, b, ca, cb, precision=None):
    return lax.dot_general(
        a, b, (((ca,), (cb,)), ((), ())), precision=precision, preferred_element_type=F32
    )


def block_of(i):
    return pl.ds(pl.multiple_of(i * LANES, LANES), LANES)


def sigmoid(v):
    return 1.0 / (1.0 + jnp.exp(-v))


def softplus(v):
    z = jnp.exp(-jnp.abs(v))
    small = z * (1.0 - z * (0.5 - z * (1.0 / 3.0 - z * 0.25)))
    return jnp.maximum(v, 0.0) + jnp.where(z < 0.01, small, jnp.log(1.0 + z))


def iota2(shape, dim):
    return lax.broadcasted_iota(jnp.int32, shape, dim)


def wide_pair(ht_ref, h):
    top = jnp.broadcast_to(ht_ref[pl.ds(h, 1), :], (HEAD_DIM, T))
    low = jnp.broadcast_to(ht_ref[pl.ds(h + 1, 1), :], (HEAD_DIM, T))
    return jnp.concatenate([top, low], axis=0).T


def main_kernel(
    counts,
    xbc_hbm, dt_ref, dy_hbm, conv_ref, head_ref,
    dx_hbm, ddt_ref, dconv_ref, dhead_ref,
    xbc_ref, dy_ref, dx_ref, load_sem, save_sem,
    ext, dms, mixed_ref, xd_ref, y_ref, dxd_ref, leave_ref, pull_ref,
    out_f, out_b, in_f, in_b, stepw_ref, headw_ref, tailw_ref,
    fade_ref, run_ref, step_ref, skip_ref, b_ref, c_ref,
    scores, dscores, db, dc, acc, halo_out, halo_in, rim_out, rim_in, tail_ref,
    packed, parts, mine, planes, total,
    send_f, recv_f, send_b, recv_b, recv_x, send_h, recv_h, send_r, recv_r,
    send_s, recv_s, send_z, recv_z, send_g, recv_g,
):
    count, depth = counts
    share = packed.shape[1] // count
    me, plane = lax.axis_index("ctx"), lax.axis_index("fsdp")
    first, last = me == 0, me == count - 1
    up = jnp.minimum(me + 1, count - 1)
    down = jnp.maximum(me - 1, 0)
    barrier = pltpu.get_barrier_semaphore()
    for r in range(1, count):
        peer = lax.rem(me + r, count)
        pl.semaphore_signal(barrier, inc=1, device_id={"ctx": peer}, device_id_type=MESH)
    for r in range(1, depth):
        peer = lax.rem(plane + r, depth)
        pl.semaphore_signal(barrier, inc=1, device_id={"fsdp": peer}, device_id_type=MESH)

    body, rest = pl.ds(0, T - TAIL), pl.ds(T - TAIL, TAIL)
    loads = [
        pltpu.make_async_copy(xbc_hbm.at[rest], xbc_ref.at[rest], load_sem.at[0]),
        pltpu.make_async_copy(xbc_hbm.at[body], xbc_ref.at[body], load_sem.at[1]),
        pltpu.make_async_copy(dy_hbm, dy_ref, load_sem.at[2]),
    ]
    for load in loads:
        load.start()

    def saves(g):
        wide = PER_GROUP * LANES
        cols = [pl.ds(pl.multiple_of(g * wide, wide), wide), block_of(PAIRS + g)]
        cols.append(block_of(PAIRS + GROUPS + g))
        return [
            pltpu.make_async_copy(dx_ref.at[body, c], dx_hbm.at[body, c], save_sem.at[g, k])
            for k, c in enumerate(cols)
        ]

    def remote(src, dst, send, recv, **to):
        return pltpu.make_async_remote_copy(
            src_ref=src, dst_ref=dst, send_sem=send, recv_sem=recv,
            device_id=to, device_id_type=MESH,
        )

    loads[0].wait()
    for i in range(BLOCKS):
        edge = xbc_ref[T - TAIL :, i * LANES : (i + 1) * LANES].astype(F32)
        halo_out[(i + BLOCKS - PAIRS) % BLOCKS] = edge[TAIL - RIM :, :]
    pl.semaphore_wait(barrier, count + depth - 2)

    def halo(k):
        rows = pl.ds(HALO_CUTS[k], HALO_CUTS[k + 1] - HALO_CUTS[k])
        return remote(halo_out.at[rows], halo_in.at[rows], send_h.at[k], recv_h.at[k], ctx=up)

    @pl.when(jnp.logical_not(last))
    def _():
        for k in range(HALOS):
            halo(k).start()

    step_th = softplus(dt_ref[...].astype(F32).T + head_ref[0:1, :])
    rate_th = step_th * (jnp.exp(head_ref[1:2, :]) * LOG2E)
    lower = (iota2((T, T), 0) >= iota2((T, T), 1)).astype(F32)
    run_ht = dot(lower, rate_th, 1, 0, lax.Precision.HIGHEST).T
    run_ref[...] = run_ht
    step_ref[...] = step_th.T
    fade_ref[...] = jnp.broadcast_to(jnp.exp2(-run_ht[:, T - 1 : T]), (HEADS, LANES))
    skip_ref[...] = jnp.broadcast_to(head_ref[2:3, :], (LANES, HEADS)).T
    acc[...] = jnp.zeros_like(acc)
    packed[...] = jnp.zeros_like(packed)
    dscores[...] = jnp.zeros_like(dscores)
    for slot in range(2):
        dms[slot, 0:8, :] = jnp.zeros((8, LANES), F32)
        dms[slot, 8 + T : 16 + T, :] = jnp.zeros((8, LANES), F32)
    causal = iota2((T, T), 0) >= iota2((T, T), 1)
    left = iota2((T, LANES), 1) < HEAD_DIM
    zero = jnp.zeros((T, LANES), BF16)

    @pl.when(first)
    def _():
        halo_in[...] = jnp.zeros_like(halo_in)

    @pl.when(jnp.logical_not(first))
    def _():
        halo(0).wait_recv()

    def split(v):
        return jnp.concatenate([jnp.where(left, v, zero), jnp.where(left, zero, v)], 0)

    def convolve(i):
        cols = block_of(i)
        ext[i, RIM : 8, :] = halo_in[lax.rem(i + BLOCKS - PAIRS, BLOCKS)]
        ext[i, 8 : 8 + T, :] = xbc_ref[:, cols].astype(F32)
        mixed = conv_ref[CONV_W : CONV_W + 1, cols] + conv_ref[0:1, cols] * ext[i, 5 : 5 + T, :]
        for j in range(1, CONV_W):
            mixed = mixed + conv_ref[j : j + 1, cols] * ext[i, 5 + j : 5 + j + T, :]
        mixed_ref[:, cols] = mixed
        return mixed * sigmoid(mixed)

    def bc(g, _):
        b16 = convolve(PAIRS + g).astype(BF16)
        c16 = convolve(PAIRS + GROUPS + g).astype(BF16)
        b_ref[:, block_of(g)] = b16
        c_ref[:, block_of(g)] = c16
        scores[g] = dot(c16, b16, 1, 1)
        return 0

    loads[1].wait()
    lax.fori_loop(0, GROUPS, bc, 0)

    def front(i):
        h = 2 * i
        g = i // PER_GROUP
        cols = block_of(i)
        x = convolve(i)
        row = [jnp.broadcast_to(run_ref[pl.ds(h + k, 1), :], (T, T)) for k in range(2)]
        col = [r.T for r in row]
        run = jnp.where(left, col[0], col[1])
        step = wide_pair(step_ref, h)
        xd = (x * step).astype(BF16)
        e_tail = jnp.exp2(run - run[T - 1 : T, :])
        e_head = jnp.exp2(-run)
        stepw_ref[:, cols] = step
        headw_ref[:, cols] = e_head
        tailw_ref[:, cols] = e_tail
        xd_ref[:, cols] = xd
        dy16 = dy_ref[:, cols]
        tail = (xd.astype(F32) * e_tail).astype(BF16)
        out = (e_head * dy16.astype(F32)).astype(BF16)
        leave_ref[cols, :] = dot(tail, b_ref[:, block_of(g)], 0, 0)
        pull_ref[cols, :] = dot(out, c_ref[:, block_of(g)], 0, 0)
        fades = [jnp.exp2(jnp.where(causal, row[k] - col[k], -1e30)) for k in range(2)]
        bd_x = split(xd)
        sc = scores[g]
        w = [(sc * f).astype(BF16) for f in fades]
        y_ref[:, cols] = dot(jnp.concatenate(w, 1), bd_x, 1, 0)
        dxd_ref[:, cols] = dot(jnp.concatenate(w, 0), split(dy16), 0, 0)
        pairwise = dot(dy16, bd_x, 1, 1)
        dscores[g] += pairwise[:, :T] * fades[0] + pairwise[:, T:] * fades[1]

    def rows_of(c):
        return pl.ds(pl.multiple_of(c * CHUNK_ROWS, CHUNK_ROWS), CHUNK_ROWS)

    def copy(c, src, dst, send, recv, peer):
        return remote(src.at[rows_of(c)], dst.at[rows_of(c)], send.at[c], recv.at[c], ctx=peer)

    cross = count // 2 - 1
    relays = count == 8
    head, foot = count - 1, 0

    def odd(c):
        return lax.rem(c, 2) == 1

    def to_relay(c, src, send, peer):
        return remote(src.at[rows_of(c)], src.at[rows_of(c)], send.at[c], recv_x.at[c], ctx=peer)

    def relay(c):
        @pl.when(last)
        def _():
            to_relay(c, out_f, send_f, foot).wait_recv()
            copy(c, out_f, in_f, send_f, recv_f, cross + 1).start()

        @pl.when(first)
        def _():
            to_relay(c, out_b, send_b, head).wait_recv()
            copy(c, out_b, in_b, send_b, recv_b, cross).start()

    def handle(c, own, src, dst, send, recv, peer, begins, ends, turns, via):
        @pl.when(begins)
        def _():
            dst[rows_of(c), :] = jnp.zeros((CHUNK_ROWS, LANES), BF16)

        @pl.when(jnp.logical_not(begins))
        def _():
            copy(c, src, dst, send, recv, peer).wait_recv()

        @pl.when(jnp.logical_not(ends))
        def _():
            for k in range(CHUNK_HEADS):
                rows = pl.ds(pl.multiple_of(c * CHUNK_ROWS + k * HEAD_DIM, HEAD_DIM), HEAD_DIM)
                fade = fade_ref[pl.ds(c * CHUNK_HEADS + k, 1), :]
                src[rows, :] = (fade * dst[rows, :].astype(F32) + own[rows, :]).astype(BF16)
            if relays:
                detour = jnp.logical_and(turns, odd(c))

                @pl.when(detour)
                def _():
                    to_relay(c, src, send, via).start()

                @pl.when(jnp.logical_not(detour))
                def _():
                    copy(c, src, dst, send, recv, peer).start()
            else:
                copy(c, src, dst, send, recv, peer).start()

    def conv_back(i, at, slot, mixed, sig, dact):
        g, k = at
        cols = block_of(i)
        dm = dact * (sig * (1.0 + mixed * (1.0 - sig)))
        dms[slot, 8 : 8 + T, :] = dm
        taps = [conv_ref[j : j + 1, cols] for j in range(CONV_W)]
        own = taps[3] * dm
        rim = taps[0] * dms[slot, 8:16, :]
        for j in range(3):
            own = own + taps[j] * dms[slot, 11 - j : 11 - j + T, :]
        for j in range(1, 3):
            rim = rim + taps[j] * dms[slot, 8 - j : 16 - j, :]
        dx_ref[:, cols] = own.astype(BF16)
        tail_ref[i] = own[T - TAIL :, :]
        rim_out[g, k] = rim[0:RIM, :]
        for j in range(CONV_W):
            packed[g, k, j : j + 1, :] = jnp.sum(dm * ext[i, 5 + j : 5 + j + T, :], 0, keepdims=True)
        packed[g, k, CONV_W : CONV_W + 1, :] = jnp.sum(dm, 0, keepdims=True)

    def pair(i, slot):
        h = 2 * i
        g = i // PER_GROUP
        cols = block_of(i)
        mixed = mixed_ref[:, cols]
        sig = sigmoid(mixed)
        x = mixed * sig
        dy = dy_ref[:, cols].astype(F32)
        step = stepw_ref[:, cols]
        xd = xd_ref[:, cols].astype(F32)
        e_tail = tailw_ref[:, cols]
        e_head = headw_ref[:, cols]
        enter = in_f[cols, :]
        later = in_b[cols, :]
        y = y_ref[:, cols] + e_head * dot(c_ref[:, block_of(g)], enter, 1, 1)
        from_tail = e_tail * dot(b_ref[:, block_of(g)], later, 1, 1)
        dxd = dxd_ref[:, cols] + from_tail
        dc[...] += dot((e_head * dy).astype(BF16), enter, 1, 0)
        db[...] += dot((xd * e_tail).astype(BF16), later, 1, 0)
        skip = jnp.where(left[0:1, :], skip_ref[pl.ds(h, 1), :], skip_ref[pl.ds(h + 1, 1), :])
        conv_back(i, (g, lax.rem(i, PER_GROUP)), slot, mixed, sig, step * dxd + skip * dy)
        both = (enter.astype(F32) * later.astype(F32)).astype(BF16)
        passed = dot(jnp.ones((8, STATE), BF16), both, 1, 1)
        sub = iota2((8, LANES), 0)
        rows = jnp.where(sub == 0, jnp.sum(dy * x, 0, keepdims=True), 0.0)
        rows = rows + jnp.where(
            sub == 1,
            jnp.sum(xd * from_tail, 0, keepdims=True) + e_head[T - 1 : T, :] * passed[0:1, :],
            0.0,
        )
        value = jnp.concatenate([xd * dxd - dy * y, x * dxd, rows], 0)
        high = value.astype(BF16)
        low = (value - high.astype(F32)).astype(BF16)
        pick = (iota2((LANES, HEADS), 1) == h + iota2((LANES, HEADS), 0) // HEAD_DIM).astype(BF16)
        acc[...] += dot(
            jnp.concatenate([high, low], 1), jnp.concatenate([pick, pick], 0), 1, 0
        )

    def piece(k):
        return pl.ds(k * share, share)

    def rim_copy(g):
        return remote(rim_out.at[g], rim_in.at[g], send_r.at[g], recv_r.at[g], ctx=down)

    def scatter(g, peer, slot):
        return remote(
            packed.at[g, piece(peer)], parts.at[g, slot],
            send_s.at[g, peer], recv_s.at[g, slot], ctx=peer,
        )

    def across(g, peer, slot):
        return remote(
            mine.at[g], planes.at[g, slot], send_z.at[g, peer], recv_z.at[g, slot], fsdp=peer
        )

    def gather(g, peer, slot):
        return remote(
            total.at[g, piece(me)], total.at[g, piece(slot)],
            send_g.at[g, peer], recv_g.at[g, slot], ctx=peer,
        )

    def share_out(g):
        for r in range(1, count):
            scatter(g, lax.rem(me + r, count), me).start()
        parts[g, me] = packed[g, piece(me)]

    def sum_ctx(g):
        for r in range(1, count):
            scatter(g, me, lax.rem(me + r, count)).wait_recv()
        own = parts[g, 0]
        for k in range(1, count):
            own = own + parts[g, k]
        mine[g] = own
        for r in range(1, depth):
            across(g, lax.rem(plane + r, depth), plane).start()
        planes[g, plane] = own

    def sum_fsdp(g):
        for r in range(1, depth):
            across(g, plane, lax.rem(plane + r, depth)).wait_recv()
        own = planes[g, 0]
        for k in range(1, depth):
            own = own + planes[g, k]
        total[g, piece(me)] = own
        for r in range(1, count):
            gather(g, lax.rem(me + r, count), me).start()

    def place(g, k):
        return jnp.where(k < PER_GROUP, g * PER_GROUP + k, PAIRS + g + (k - PER_GROUP) * GROUPS)

    def finish(g):
        for r in range(1, count):
            gather(g, me, lax.rem(me + r, count)).wait_recv()

        def spread(k, _):
            dconv_ref[:, block_of(place(g, k))] = total[g, k, 0 : CONV_W + 1, :]
            return 0

        lax.fori_loop(0, GROUP_BLOCKS, spread, 0)

    def seam(g):
        @pl.when(jnp.logical_not(last))
        def _():
            rim_copy(g).wait_recv()

            def fix(k, _):
                i = place(g, k)
                pad = jnp.zeros((TAIL - (CONV_W - 1), LANES), F32)
                moved = jnp.concatenate([pad, rim_in[g, k][0 : CONV_W - 1, :]], 0)
                dx_ref[T - TAIL :, block_of(i)] = (tail_ref[i] + moved).astype(BF16)
                return 0

            lax.fori_loop(0, GROUP_BLOCKS, fix, 0)

    def close_group(g):
        ds = dscores[g].astype(BF16)
        b16 = b_ref[:, block_of(g)]
        c16 = c_ref[:, block_of(g)]
        for slot, k, at, sums in (
            (0, PER_GROUP, PAIRS + g, db[...] + dot(ds, c16, 0, 0)),
            (1, PER_GROUP + 1, PAIRS + GROUPS + g, dc[...] + dot(ds, b16, 1, 0)),
        ):
            mixed = mixed_ref[:, block_of(at)]
            conv_back(at, (g, k), slot, mixed, sigmoid(mixed), sums)

        @pl.when(jnp.logical_not(first))
        def _():
            rim_copy(g).start()

        for save in saves(g):
            save.start()

    def lag(place):
        steps = (place + 1) // 2 * LAG_CORE + place // 2 * LAG_CHIP
        return steps + place // (count // 2) * (LAG_CROSS - LAG_CHIP) if relays else steps

    lag_f, lag_b = lag(me), lag(count - 1 - me)
    delay = jnp.maximum(lag_f, lag_b)
    longest = lag(count - 1)

    def phase(v, wait, act, most=GROUPS - 1):
        q = v - (longest + GROUP_CHUNKS - 1 + wait)
        g = q // GROUP_CHUNKS

        @pl.when(jnp.logical_and(q >= 0, jnp.logical_and(lax.rem(q, GROUP_CHUNKS) == 0, g < most)))
        def _():
            act(g)

    def fronts(c):
        for k in range(CHUNK_PAIRS):
            front(c * CHUNK_PAIRS + k)

    loads[2].wait()
    fronts(0)

    def tick(v, _):
        c = v - lag_f
        if relays:
            e = v - lag(cross) - LAG_RELAY

            @pl.when(jnp.logical_and(jnp.logical_and(e >= 0, e < CHUNKS), odd(e)))
            def _():
                relay(e)

        for q in range(1, HALOS):
            @pl.when(jnp.logical_and(v == (HALO_CUTS[q] + PAIRS - BLOCKS) // CHUNK_PAIRS - 1, jnp.logical_not(first)))
            def _():
                halo(q).wait_recv()

        @pl.when(jnp.logical_and(c >= 0, c < CHUNKS))
        def _():
            handle(c, leave_ref, out_f, in_f, send_f, recv_f, up, first, last, me == cross, head)

        d = v - lag_b

        @pl.when(jnp.logical_and(d >= 0, d < CHUNKS))
        def _():
            handle(d, pull_ref, out_b, in_b, send_b, recv_b, down, last, first, me == cross + 1, foot)

        @pl.when(v + 1 < CHUNKS)
        def _():
            fronts(v + 1)

        w = v - delay
        inside = jnp.logical_and(w >= 0, w < CHUNKS)

        @pl.when(jnp.logical_and(inside, lax.rem(w, GROUP_CHUNKS) == 0))
        def _():
            db[...] = jnp.zeros_like(db)
            dc[...] = jnp.zeros_like(dc)

        @pl.when(inside)
        def _():
            for k in range(CHUNK_PAIRS):
                pair(w * CHUNK_PAIRS + k, k)

        @pl.when(jnp.logical_and(inside, lax.rem(w, GROUP_CHUNKS) == GROUP_CHUNKS - 1))
        def _():
            g = w // GROUP_CHUNKS
            close_group(g)

            @pl.when(g < GROUPS - 1)
            def _():
                share_out(g)

        phase(v, 4, sum_ctx)
        phase(v, 5, seam)
        phase(v, 8, sum_fsdp, GROUPS - 2)
        return 0

    lax.fori_loop(0, CHUNKS + longest, tick, 0)

    upper = (iota2((T, T), 0) <= iota2((T, T), 1)).astype(F32)
    d_rate = dot(upper, acc[0:T, :], 1, 0, lax.Precision.HIGHEST) - acc[2 * T + 1 : 2 * T + 2, :]
    scale = jnp.exp(head_ref[1:2, :])
    raw = dt_ref[...].astype(F32).T + head_ref[0:1, :]
    d_dt = (acc[T : 2 * T, :] + d_rate * scale) * sigmoid(raw)
    end = GROUPS - 1
    packed[end, GROUP_BLOCKS, 0:1, :] = jnp.sum(d_dt, 0, keepdims=True)
    packed[end, GROUP_BLOCKS, 1:2, :] = jnp.sum(d_rate * softplus(raw) * scale, 0, keepdims=True)
    packed[end, GROUP_BLOCKS, 2:3, :] = acc[2 * T : 2 * T + 1, :]
    share_out(end)
    ddt_ref[...] = d_dt.T
    sum_ctx(end)
    sum_fsdp(end - 1)
    seam(end)
    last_rows = pltpu.make_async_copy(dx_ref.at[rest], dx_hbm.at[rest], load_sem.at[0])
    last_rows.start()

    def drain(c, _):
        passes = jnp.logical_and(relays, odd(c))

        @pl.when(jnp.logical_or(jnp.logical_not(last), passes))
        def _():
            copy(c, out_f, in_f, send_f, recv_f, up).wait_send()

        @pl.when(jnp.logical_or(jnp.logical_not(first), passes))
        def _():
            copy(c, out_b, in_b, send_b, recv_b, down).wait_send()

        return 0

    lax.fori_loop(0, CHUNKS, drain, 0)

    @pl.when(jnp.logical_not(last))
    def _():
        for k in range(HALOS):
            halo(k).wait_send()

    def settle(g, _):
        for save in saves(g):
            save.wait()
        for r in range(1, count):
            scatter(g, lax.rem(me + r, count), me).wait_send()
        for r in range(1, depth):
            across(g, lax.rem(plane + r, depth), plane).wait_send()

        @pl.when(jnp.logical_not(first))
        def _():
            rim_copy(g).wait_send()

        return 0

    lax.fori_loop(0, GROUPS, settle, 0)
    sum_fsdp(end)
    for g in range(GROUPS):
        finish(g)
    last_rows.wait()
    dhead_ref[...] = total[end, GROUP_BLOCKS, 0:3, :]

    def settle_last(g, _):
        for r in range(1, count):
            gather(g, lax.rem(me + r, count), me).wait_send()
        return 0

    lax.fori_loop(0, GROUPS, settle_last, 0)


def land_kernel(*refs):
    n = (len(refs) - 2) // 3
    ins, outs, held = refs[:n], refs[n : 2 * n], refs[2 * n : 3 * n]
    in_sem, out_sem = refs[3 * n :]
    rows = T // LANDINGS
    parts = [(0, pl.ds(k * rows, rows)) for k in range(LANDINGS)]
    parts += [(k, pl.ds(0, ins[k].shape[0])) for k in range(1, n)]

    def arrive(s):
        k, r = parts[s]
        return pltpu.make_async_copy(ins[k].at[r], held[k].at[r], in_sem.at[s])

    def leave(s):
        k, r = parts[s]
        return pltpu.make_async_copy(held[k].at[r], outs[k].at[r], out_sem.at[s])

    for s in range(len(parts)):
        arrive(s).start()
    for s in range(len(parts)):
        arrive(s).wait()
        leave(s).start()
    for s in range(len(parts)):
        leave(s).wait()


def spots(count, far):
    return [pl.BlockSpec(memory_space=pl.ANY if k in far else pltpu.VMEM) for k in range(count)]


def call(kernel, out, scratch, args, limit, far_in, far_out, **params):
    return pl.pallas_call(
        kernel,
        out_shape=[jax.ShapeDtypeStruct(s, d) for s, d in out],
        in_specs=spots(len(args), far_in),
        out_specs=spots(len(out), far_out),
        scratch_shapes=scratch,
        compiler_params=pltpu.CompilerParams(vmem_limit_bytes=limit << 20, **params),
    )(*args)


def shards(xbc, dt_raw, dy, conv_params, head_params):
    count, depth = lax.axis_size("ctx"), lax.axis_size("fsdp")
    share = pl.cdiv(GROUP_BLOCKS + 1, count)
    wide, wide16 = pltpu.VMEM((T, X_WIDTH), F32), pltpu.VMEM((T, X_WIDTH), BF16)
    tall, tall16 = pltpu.VMEM((X_WIDTH, STATE), F32), pltpu.VMEM((X_WIDTH, STATE), BF16)
    small = pltpu.VMEM((T, LANES), F32)
    narrow = pltpu.VMEM((T, GROUPS * STATE), BF16)
    square = pltpu.VMEM((GROUPS, T, T), F32)
    edge = pltpu.VMEM((BLOCKS, RIM, LANES), F32)
    rim = pltpu.VMEM((GROUPS, GROUP_BLOCKS, RIM, LANES), F32)
    whole = pltpu.VMEM((GROUPS, share * count, 8, LANES), F32)
    dma = pltpu.SemaphoreType.DMA
    dx, ddt, dconv, dhead = call(
        functools.partial(main_kernel, (count, depth)),
        [((T, CHANNELS), BF16), ((HEADS, T), F32), ((CONV_W + 1, CHANNELS), F32), ((3, HEADS), F32)],
        [pltpu.VMEM((T, CHANNELS), BF16), wide16, pltpu.VMEM((T, CHANNELS), BF16),
         dma((3,)), dma((GROUPS, 3)),
         pltpu.VMEM((BLOCKS, 8 + T, LANES), F32), pltpu.VMEM((2, 16 + T, LANES), F32),
         pltpu.VMEM((T, CHANNELS), F32), wide16, wide, wide, tall, tall,
         tall16, tall16, tall16, tall16, wide, wide, wide,
         small, small, small, small, narrow, narrow,
         square, square, small, small, pltpu.VMEM((2 * T + 8, HEADS), F32),
         edge, edge, rim, rim, pltpu.VMEM((BLOCKS, TAIL, LANES), F32),
         whole, pltpu.VMEM((GROUPS, count, share, 8, LANES), F32),
         pltpu.VMEM((GROUPS, share, 8, LANES), F32),
         pltpu.VMEM((GROUPS, depth, share, 8, LANES), F32), whole]
        + [dma((CHUNKS,))] * 5 + [dma((HALOS,))] * 2 + [dma((GROUPS,))] * 2
        + [dma((GROUPS, count))] * 2 + [dma((GROUPS, depth))] * 2 + [dma((GROUPS, count))] * 2,
        (xbc[0], dt_raw[0], dy[0], conv_params, head_params),
        far_in=(0, 2),
        far_out=(0,),
        limit=63,
        collective_id=0,
        has_side_effects=True,
    )
    results = (dx, ddt, dconv, dhead)
    anywhere = [pl.BlockSpec(memory_space=pl.ANY)] * len(results)
    dx, ddt, dconv, dhead = pl.pallas_call(
        land_kernel,
        out_shape=[jax.ShapeDtypeStruct(r.shape, r.dtype) for r in results],
        in_specs=anywhere,
        out_specs=anywhere,
        scratch_shapes=[pltpu.VMEM(r.shape, r.dtype) for r in results]
        + [dma((LANDINGS + len(results) - 1,))] * 2,
    )(*results)
    return dx[None], ddt[None], dconv, dhead


def solution(mesh):
    return jax.shard_map(
        shards,
        mesh=mesh,
        in_specs=(P("fsdp", "ctx", None), P("fsdp", None, "ctx"), P("fsdp", "ctx", None), P(), P()),
        out_specs=(P("fsdp", "ctx", None), P("fsdp", None, "ctx"), P(), P()),
        check_vma=False,
    )
```

```python
import functools

import jax
import jax.numpy as jnp
from jax import lax
from jax.experimental import pallas as pl
from jax.experimental.pallas import tpu as pltpu
from jax.sharding import PartitionSpec as P

HEADS = 128
HEAD_DIM = 64
STATE = 128
GROUPS = 4
CONV_W = 4
T = 128
LANES = 128
X_WIDTH = HEADS * HEAD_DIM
CHANNELS = X_WIDTH + 2 * GROUPS * STATE
PAIRS = HEADS // 2
PER_GROUP = PAIRS // GROUPS
F32 = jnp.float32
BF16 = jnp.bfloat16
MESH = pl.DeviceIdType.MESH
CHUNKS = 32
CHUNK_HEADS = HEADS // CHUNKS
CHUNK_ROWS = X_WIDTH // CHUNKS
CHUNK_PAIRS = PAIRS // CHUNKS
GROUP_CHUNKS = CHUNKS // GROUPS
LAG_CORE = 2
LAG_CHIP = 5
LAG_CROSS = 9
TAIL = 16
LANDINGS = 8
RIM = 4
HALO_CUTS = (0, 16, 40, 72)
HALOS = len(HALO_CUTS) - 1
BLOCKS = CHANNELS // LANES
GROUP_BLOCKS = PER_GROUP + 2
LOG2E = 1.4426950408889634


def dot(a, b, ca, cb, precision=None):
    return lax.dot_general(
        a, b, (((ca,), (cb,)), ((), ())), precision=precision, preferred_element_type=F32
    )


def block_of(i):
    return pl.ds(pl.multiple_of(i * LANES, LANES), LANES)


def sigmoid(v):
    return 1.0 / (1.0 + jnp.exp(-v))


def softplus(v):
    z = jnp.exp(-jnp.abs(v))
    small = z * (1.0 - z * (0.5 - z * (1.0 / 3.0 - z * 0.25)))
    return jnp.maximum(v, 0.0) + jnp.where(z < 0.01, small, jnp.log(1.0 + z))


def iota2(shape, dim):
    return lax.broadcasted_iota(jnp.int32, shape, dim)


def wide_pair(ht_ref, h):
    top = jnp.broadcast_to(ht_ref[pl.ds(h, 1), :], (HEAD_DIM, T))
    low = jnp.broadcast_to(ht_ref[pl.ds(h + 1, 1), :], (HEAD_DIM, T))
    return jnp.concatenate([top, low], axis=0).T


def main_kernel(
    counts,
    xbc_hbm, dt_ref, dy_hbm, conv_ref, head_ref,
    dx_hbm, ddt_ref, dconv_ref, dhead_ref,
    xbc_ref, dy_ref, dx_ref, load_sem, save_sem,
    ext, dms, mixed_ref, xd_ref, y_ref, dxd_ref, leave_ref, pull_ref,
    out_f, out_b, in_f, in_b, stepw_ref, headw_ref, tailw_ref,
    fade_ref, run_ref, step_ref, skip_ref, b_ref, c_ref,
    scores, dscores, db, dc, acc, halo_out, halo_in, rim_out, rim_in, tail_ref,
    packed, parts, mine, planes, total,
    extra, fade_in, fade_out,
    send_f, recv_f, send_b, recv_b, recv_x, also_f, also_b, fade_sem, send_h, recv_h, send_r, recv_r,
    send_s, recv_s, send_z, recv_z, send_g, recv_g,
):
    count, depth = counts
    share = packed.shape[1] // count
    me, plane = lax.axis_index("ctx"), lax.axis_index("fsdp")
    first, last = me == 0, me == count - 1
    up = jnp.minimum(me + 1, count - 1)
    down = jnp.maximum(me - 1, 0)
    barrier = pltpu.get_barrier_semaphore()
    for r in range(1, count):
        peer = lax.rem(me + r, count)
        pl.semaphore_signal(barrier, inc=1, device_id={"ctx": peer}, device_id_type=MESH)
    for r in range(1, depth):
        peer = lax.rem(plane + r, depth)
        pl.semaphore_signal(barrier, inc=1, device_id={"fsdp": peer}, device_id_type=MESH)

    body, rest = pl.ds(0, T - TAIL), pl.ds(T - TAIL, TAIL)
    loads = [
        pltpu.make_async_copy(xbc_hbm.at[rest], xbc_ref.at[rest], load_sem.at[0]),
        pltpu.make_async_copy(xbc_hbm.at[body], xbc_ref.at[body], load_sem.at[1]),
        pltpu.make_async_copy(dy_hbm, dy_ref, load_sem.at[2]),
    ]
    for load in loads:
        load.start()

    def saves(g):
        wide = PER_GROUP * LANES
        cols = [pl.ds(pl.multiple_of(g * wide, wide), wide), block_of(PAIRS + g)]
        cols.append(block_of(PAIRS + GROUPS + g))
        return [
            pltpu.make_async_copy(dx_ref.at[body, c], dx_hbm.at[body, c], save_sem.at[g, k])
            for k, c in enumerate(cols)
        ]

    def remote(src, dst, send, recv, **to):
        return pltpu.make_async_remote_copy(
            src_ref=src, dst_ref=dst, send_sem=send, recv_sem=recv,
            device_id=to, device_id_type=MESH,
        )

    loads[0].wait()
    for i in range(BLOCKS):
        edge = xbc_ref[T - TAIL :, i * LANES : (i + 1) * LANES].astype(F32)
        halo_out[(i + BLOCKS - PAIRS) % BLOCKS] = edge[TAIL - RIM :, :]
    pl.semaphore_wait(barrier, count + depth - 2)

    def halo(k):
        rows = pl.ds(HALO_CUTS[k], HALO_CUTS[k + 1] - HALO_CUTS[k])
        return remote(halo_out.at[rows], halo_in.at[rows], send_h.at[k], recv_h.at[k], ctx=up)

    @pl.when(jnp.logical_not(last))
    def _():
        for k in range(HALOS):
            halo(k).start()

    step_th = softplus(dt_ref[...].astype(F32).T + head_ref[0:1, :])
    rate_th = step_th * (jnp.exp(head_ref[1:2, :]) * LOG2E)
    lower = (iota2((T, T), 0) >= iota2((T, T), 1)).astype(F32)
    run_ht = dot(lower, rate_th, 1, 0, lax.Precision.HIGHEST).T
    run_ref[...] = run_ht
    step_ref[...] = step_th.T
    fade_ref[...] = jnp.broadcast_to(jnp.exp2(-run_ht[:, T - 1 : T]), (HEADS, LANES))
    skip_ref[...] = jnp.broadcast_to(head_ref[2:3, :], (LANES, HEADS)).T
    acc[...] = jnp.zeros_like(acc)
    packed[...] = jnp.zeros_like(packed)
    dscores[...] = jnp.zeros_like(dscores)
    for slot in range(2):
        dms[slot, 0:8, :] = jnp.zeros((8, LANES), F32)
        dms[slot, 8 + T : 16 + T, :] = jnp.zeros((8, LANES), F32)
    causal = iota2((T, T), 0) >= iota2((T, T), 1)
    left = iota2((T, LANES), 1) < HEAD_DIM
    zero = jnp.zeros((T, LANES), BF16)

    @pl.when(first)
    def _():
        halo_in[...] = jnp.zeros_like(halo_in)

    @pl.when(jnp.logical_not(first))
    def _():
        halo(0).wait_recv()

    def split(v):
        return jnp.concatenate([jnp.where(left, v, zero), jnp.where(left, zero, v)], 0)

    def convolve(i):
        cols = block_of(i)
        ext[i, RIM : 8, :] = halo_in[lax.rem(i + BLOCKS - PAIRS, BLOCKS)]
        ext[i, 8 : 8 + T, :] = xbc_ref[:, cols].astype(F32)
        mixed = conv_ref[CONV_W : CONV_W + 1, cols] + conv_ref[0:1, cols] * ext[i, 5 : 5 + T, :]
        for j in range(1, CONV_W):
            mixed = mixed + conv_ref[j : j + 1, cols] * ext[i, 5 + j : 5 + j + T, :]
        mixed_ref[:, cols] = mixed
        return mixed * sigmoid(mixed)

    def bc(g, _):
        b16 = convolve(PAIRS + g).astype(BF16)
        c16 = convolve(PAIRS + GROUPS + g).astype(BF16)
        b_ref[:, block_of(g)] = b16
        c_ref[:, block_of(g)] = c16
        scores[g] = dot(c16, b16, 1, 1)
        return 0

    loads[1].wait()
    lax.fori_loop(0, GROUPS, bc, 0)

    def front(i):
        h = 2 * i
        g = i // PER_GROUP
        cols = block_of(i)
        x = convolve(i)
        row = [jnp.broadcast_to(run_ref[pl.ds(h + k, 1), :], (T, T)) for k in range(2)]
        col = [r.T for r in row]
        run = jnp.where(left, col[0], col[1])
        step = wide_pair(step_ref, h)
        xd = (x * step).astype(BF16)
        e_tail = jnp.exp2(run - run[T - 1 : T, :])
        e_head = jnp.exp2(-run)
        stepw_ref[:, cols] = step
        headw_ref[:, cols] = e_head
        tailw_ref[:, cols] = e_tail
        xd_ref[:, cols] = xd
        dy16 = dy_ref[:, cols]
        tail = (xd.astype(F32) * e_tail).astype(BF16)
        out = (e_head * dy16.astype(F32)).astype(BF16)
        leave_ref[cols, :] = dot(tail, b_ref[:, block_of(g)], 0, 0)
        pull_ref[cols, :] = dot(out, c_ref[:, block_of(g)], 0, 0)
        fades = [jnp.exp2(jnp.where(causal, row[k] - col[k], -1e30)) for k in range(2)]
        bd_x = split(xd)
        sc = scores[g]
        w = [(sc * f).astype(BF16) for f in fades]
        y_ref[:, cols] = dot(jnp.concatenate(w, 1), bd_x, 1, 0)
        dxd_ref[:, cols] = dot(jnp.concatenate(w, 0), split(dy16), 0, 0)
        pairwise = dot(dy16, bd_x, 1, 1)
        dscores[g] += pairwise[:, :T] * fades[0] + pairwise[:, T:] * fades[1]

    def rows_of(c):
        return pl.ds(pl.multiple_of(c * CHUNK_ROWS, CHUNK_ROWS), CHUNK_ROWS)

    def copy(c, src, dst, send, recv, peer):
        return remote(src.at[rows_of(c)], dst.at[rows_of(c)], send.at[c], recv.at[c], ctx=peer)

    routed = count == 8

    def odd(c):
        return lax.rem(c, 2) == 1

    def blend(c, dst, fades, src, base):
        for k in range(CHUNK_HEADS):
            rows = pl.ds(pl.multiple_of(c * CHUNK_ROWS + k * HEAD_DIM, HEAD_DIM), HEAD_DIM)
            fade = fades[pl.ds(c * CHUNK_HEADS + k, 1), :]
            mixed = fade * src[rows, :].astype(F32) + base[rows, :].astype(F32)
            dst[rows, :] = mixed.astype(BF16)

    def handle(c, own, src, dst, send, recv, peer, begins, ends):
        @pl.when(begins)
        def _():
            dst[rows_of(c), :] = jnp.zeros((CHUNK_ROWS, LANES), BF16)

        @pl.when(jnp.logical_not(begins))
        def _():
            copy(c, src, dst, send, recv, peer).wait_recv()

        @pl.when(jnp.logical_not(ends))
        def _():
            blend(c, src, fade_ref, dst, own)
            copy(c, src, dst, send, recv, peer).start()

    t3 = 2 * LAG_CORE + LAG_CHIP
    t4, t6 = t3 + LAG_CROSS, t3 + LAG_CHIP
    table = (0, LAG_CORE, LAG_CORE + LAG_CHIP, t3, t4, t4 + LAG_CORE, t6, t6 + LAG_CORE)

    def fade_hop(src, send, peer):
        return remote(src, fade_in, send, fade_sem.at[2], ctx=peer)

    def chain(own, out, inn, send, also, recv, role, dev):
        def go(c, src, dst, send, recv, r):
            return copy(c, src, dst, send, recv, dev(r))

        def fades():
            @pl.when(role == 4)
            def _():
                fade_hop(fade_ref, fade_sem.at[0], dev(5)).start()

        def fades_end():
            @pl.when(role == 4)
            def _():
                fade_hop(fade_ref, fade_sem.at[0], dev(5)).wait_send()

            @pl.when(role == 5)
            def _():
                fade_hop(fade_out, fade_sem.at[1], dev(6)).wait_send()

        def early(v):
            @pl.when(jnp.logical_and(role == 4, v < CHUNKS))
            def _():
                extra[rows_of(v), :] = own[rows_of(v), :].astype(BF16)
                go(v, extra, extra, also, recv_x, 5).start()

            q = v - LAG_CORE

            @pl.when(jnp.logical_and(role == 5, q == 0))
            def _():
                fade_hop(fade_ref, fade_sem.at[0], dev(4)).wait_recv()
                fade_out[...] = fade_in[...] * fade_ref[...]
                fade_hop(fade_out, fade_sem.at[1], dev(6)).start()

            @pl.when(jnp.logical_and(role == 5, jnp.logical_and(q >= 0, q < CHUNKS)))
            def _():
                go(q, extra, extra, also, recv_x, 4).wait_recv()
                blend(q, out, fade_ref, extra, own)
                go(q, out, inn, send, recv, 6).start()

        def late(c):
            @pl.when(role == 0)
            def _():
                inn[rows_of(c), :] = jnp.zeros((CHUNK_ROWS, LANES), BF16)

            @pl.when(jnp.logical_and(role == 6, c == 0))
            def _():
                fade_hop(fade_out, fade_sem.at[1], dev(5)).wait_recv()

            @pl.when(role == 6)
            def _():
                go(c, out, extra, send, recv_x, 3).wait_recv()

                @pl.when(odd(c))
                def _():
                    go(c, extra, inn, also, recv, 4).start()

            @pl.when(role > 0)
            def _():
                go(c, out, inn, send, recv, 0).wait_recv()

            @pl.when(role == 6)
            def _():
                blend(c, inn, fade_in, extra, inn)

            @pl.when(jnp.logical_and(role != 5, role != 7))
            def _():
                blend(c, out, fade_ref, inn, own)

                @pl.when(role != 3)
                def _():
                    copy(c, out, inn, send, recv, dev(role + 1)).start()

                @pl.when(role == 3)
                def _():
                    go(c, out, extra, send, recv_x, 6).start()

                    @pl.when(jnp.logical_not(odd(c)))
                    def _():
                        go(c, out, inn, also, recv, 4).start()

        def sent(c):
            @pl.when(role != 7)
            def _():
                go(c, out, inn, send, recv, 7).wait_send()

            second = jnp.logical_and(role == 3, jnp.logical_not(odd(c)))
            second = jnp.logical_or(second, jnp.logical_and(role == 6, odd(c)))

            @pl.when(jnp.logical_or(role == 4, second))
            def _():
                go(c, extra, inn, also, recv, 7).wait_send()

        return fades, early, late, sent, fades_end

    def ahead(role):
        return role

    def behind(role):
        return count - 1 - role

    chains = (
        chain(leave_ref, out_f, in_f, send_f, also_f, recv_f, me, ahead),
        chain(pull_ref, out_b, in_b, send_b, also_b, recv_b, count - 1 - me, behind),
    )

    def conv_back(i, at, slot, mixed, sig, dact):
        g, k = at
        cols = block_of(i)
        dm = dact * (sig * (1.0 + mixed * (1.0 - sig)))
        dms[slot, 8 : 8 + T, :] = dm
        taps = [conv_ref[j : j + 1, cols] for j in range(CONV_W)]
        own = taps[3] * dm
        rim = taps[0] * dms[slot, 8:16, :]
        for j in range(3):
            own = own + taps[j] * dms[slot, 11 - j : 11 - j + T, :]
        for j in range(1, 3):
            rim = rim + taps[j] * dms[slot, 8 - j : 16 - j, :]
        dx_ref[:, cols] = own.astype(BF16)
        tail_ref[i] = own[T - TAIL :, :]
        rim_out[g, k] = rim[0:RIM, :]
        for j in range(CONV_W):
            packed[g, k, j : j + 1, :] = jnp.sum(dm * ext[i, 5 + j : 5 + j + T, :], 0, keepdims=True)
        packed[g, k, CONV_W : CONV_W + 1, :] = jnp.sum(dm, 0, keepdims=True)

    def pair(i, slot):
        h = 2 * i
        g = i // PER_GROUP
        cols = block_of(i)
        mixed = mixed_ref[:, cols]
        sig = sigmoid(mixed)
        x = mixed * sig
        dy = dy_ref[:, cols].astype(F32)
        step = stepw_ref[:, cols]
        xd = xd_ref[:, cols].astype(F32)
        e_tail = tailw_ref[:, cols]
        e_head = headw_ref[:, cols]
        enter = in_f[cols, :]
        later = in_b[cols, :]
        y = y_ref[:, cols] + e_head * dot(c_ref[:, block_of(g)], enter, 1, 1)
        from_tail = e_tail * dot(b_ref[:, block_of(g)], later, 1, 1)
        dxd = dxd_ref[:, cols] + from_tail
        dc[...] += dot((e_head * dy).astype(BF16), enter, 1, 0)
        db[...] += dot((xd * e_tail).astype(BF16), later, 1, 0)
        skip = jnp.where(left[0:1, :], skip_ref[pl.ds(h, 1), :], skip_ref[pl.ds(h + 1, 1), :])
        conv_back(i, (g, lax.rem(i, PER_GROUP)), slot, mixed, sig, step * dxd + skip * dy)
        both = (enter.astype(F32) * later.astype(F32)).astype(BF16)
        passed = dot(jnp.ones((8, STATE), BF16), both, 1, 1)
        sub = iota2((8, LANES), 0)
        rows = jnp.where(sub == 0, jnp.sum(dy * x, 0, keepdims=True), 0.0)
        rows = rows + jnp.where(
            sub == 1,
            jnp.sum(xd * from_tail, 0, keepdims=True) + e_head[T - 1 : T, :] * passed[0:1, :],
            0.0,
        )
        value = jnp.concatenate([xd * dxd - dy * y, x * dxd, rows], 0)
        high = value.astype(BF16)
        low = (value - high.astype(F32)).astype(BF16)
        pick = (iota2((LANES, HEADS), 1) == h + iota2((LANES, HEADS), 0) // HEAD_DIM).astype(BF16)
        acc[...] += dot(
            jnp.concatenate([high, low], 1), jnp.concatenate([pick, pick], 0), 1, 0
        )

    def piece(k):
        return pl.ds(k * share, share)

    def rim_copy(g):
        return remote(rim_out.at[g], rim_in.at[g], send_r.at[g], recv_r.at[g], ctx=down)

    def scatter(g, peer, slot):
        return remote(
            packed.at[g, piece(peer)], parts.at[g, slot],
            send_s.at[g, peer], recv_s.at[g, slot], ctx=peer,
        )

    def across(g, peer, slot):
        return remote(
            mine.at[g], planes.at[g, slot], send_z.at[g, peer], recv_z.at[g, slot], fsdp=peer
        )

    def gather(g, peer, slot):
        return remote(
            total.at[g, piece(me)], total.at[g, piece(slot)],
            send_g.at[g, peer], recv_g.at[g, slot], ctx=peer,
        )

    def share_out(g):
        for r in range(1, count):
            scatter(g, lax.rem(me + r, count), me).start()
        parts[g, me] = packed[g, piece(me)]

    def sum_ctx(g):
        for r in range(1, count):
            scatter(g, me, lax.rem(me + r, count)).wait_recv()
        own = parts[g, 0]
        for k in range(1, count):
            own = own + parts[g, k]
        mine[g] = own
        for r in range(1, depth):
            across(g, lax.rem(plane + r, depth), plane).start()
        planes[g, plane] = own

    def sum_fsdp(g):
        for r in range(1, depth):
            across(g, plane, lax.rem(plane + r, depth)).wait_recv()
        own = planes[g, 0]
        for k in range(1, depth):
            own = own + planes[g, k]
        total[g, piece(me)] = own
        for r in range(1, count):
            gather(g, lax.rem(me + r, count), me).start()

    def place(g, k):
        return jnp.where(k < PER_GROUP, g * PER_GROUP + k, PAIRS + g + (k - PER_GROUP) * GROUPS)

    def finish(g):
        for r in range(1, count):
            gather(g, me, lax.rem(me + r, count)).wait_recv()

        def spread(k, _):
            dconv_ref[:, block_of(place(g, k))] = total[g, k, 0 : CONV_W + 1, :]
            return 0

        lax.fori_loop(0, GROUP_BLOCKS, spread, 0)

    def seam(g):
        @pl.when(jnp.logical_not(last))
        def _():
            rim_copy(g).wait_recv()

            def fix(k, _):
                i = place(g, k)
                pad = jnp.zeros((TAIL - (CONV_W - 1), LANES), F32)
                moved = jnp.concatenate([pad, rim_in[g, k][0 : CONV_W - 1, :]], 0)
                dx_ref[T - TAIL :, block_of(i)] = (tail_ref[i] + moved).astype(BF16)
                return 0

            lax.fori_loop(0, GROUP_BLOCKS, fix, 0)

    def close_group(g):
        ds = dscores[g].astype(BF16)
        b16 = b_ref[:, block_of(g)]
        c16 = c_ref[:, block_of(g)]
        for slot, k, at, sums in (
            (0, PER_GROUP, PAIRS + g, db[...] + dot(ds, c16, 0, 0)),
            (1, PER_GROUP + 1, PAIRS + GROUPS + g, dc[...] + dot(ds, b16, 1, 0)),
        ):
            mixed = mixed_ref[:, block_of(at)]
            conv_back(at, (g, k), slot, mixed, sigmoid(mixed), sums)

        @pl.when(jnp.logical_not(first))
        def _():
            rim_copy(g).start()

        for save in saves(g):
            save.start()

    def lag(place):
        if routed:
            return sum(jnp.where(place == k, at, 0) for k, at in enumerate(table))
        return (place + 1) // 2 * LAG_CORE + place // 2 * LAG_CHIP

    lag_f, lag_b = lag(me), lag(count - 1 - me)
    delay = jnp.maximum(lag_f, lag_b)
    longest = max(table) if routed else lag(count - 1)

    def phase(v, wait, act, most=GROUPS - 1):
        q = v - (longest + GROUP_CHUNKS - 1 + wait)
        g = q // GROUP_CHUNKS

        @pl.when(jnp.logical_and(q >= 0, jnp.logical_and(lax.rem(q, GROUP_CHUNKS) == 0, g < most)))
        def _():
            act(g)

    def fronts(c):
        for k in range(CHUNK_PAIRS):
            front(c * CHUNK_PAIRS + k)

    loads[2].wait()
    fronts(0)
    if routed:
        chains[0][0]()
        chains[1][0]()

    def tick(v, _):
        for q in range(1, HALOS):
            @pl.when(jnp.logical_and(v == (HALO_CUTS[q] + PAIRS - BLOCKS) // CHUNK_PAIRS - 1, jnp.logical_not(first)))
            def _():
                halo(q).wait_recv()

        c, d = v - lag_f, v - lag_b
        active_f = jnp.logical_and(c >= 0, c < CHUNKS)
        active_b = jnp.logical_and(d >= 0, d < CHUNKS)
        if routed:
            chains[0][1](v)
            chains[1][1](v)

        @pl.when(active_f)
        def _():
            if routed:
                chains[0][2](c)
            else:
                handle(c, leave_ref, out_f, in_f, send_f, recv_f, up, first, last)

        @pl.when(active_b)
        def _():
            if routed:
                chains[1][2](d)
            else:
                handle(d, pull_ref, out_b, in_b, send_b, recv_b, down, last, first)

        @pl.when(v + 1 < CHUNKS)
        def _():
            fronts(v + 1)

        w = v - delay
        inside = jnp.logical_and(w >= 0, w < CHUNKS)

        @pl.when(jnp.logical_and(inside, lax.rem(w, GROUP_CHUNKS) == 0))
        def _():
            db[...] = jnp.zeros_like(db)
            dc[...] = jnp.zeros_like(dc)

        @pl.when(inside)
        def _():
            for k in range(CHUNK_PAIRS):
                pair(w * CHUNK_PAIRS + k, k)

        @pl.when(jnp.logical_and(inside, lax.rem(w, GROUP_CHUNKS) == GROUP_CHUNKS - 1))
        def _():
            g = w // GROUP_CHUNKS
            close_group(g)

            @pl.when(g < GROUPS - 1)
            def _():
                share_out(g)

        phase(v, 4, sum_ctx)
        phase(v, 5, seam)
        phase(v, 8, sum_fsdp, GROUPS - 2)
        return 0

    lax.fori_loop(0, CHUNKS + longest, tick, 0)

    upper = (iota2((T, T), 0) <= iota2((T, T), 1)).astype(F32)
    d_rate = dot(upper, acc[0:T, :], 1, 0, lax.Precision.HIGHEST) - acc[2 * T + 1 : 2 * T + 2, :]
    scale = jnp.exp(head_ref[1:2, :])
    raw = dt_ref[...].astype(F32).T + head_ref[0:1, :]
    d_dt = (acc[T : 2 * T, :] + d_rate * scale) * sigmoid(raw)
    end = GROUPS - 1
    packed[end, GROUP_BLOCKS, 0:1, :] = jnp.sum(d_dt, 0, keepdims=True)
    packed[end, GROUP_BLOCKS, 1:2, :] = jnp.sum(d_rate * softplus(raw) * scale, 0, keepdims=True)
    packed[end, GROUP_BLOCKS, 2:3, :] = acc[2 * T : 2 * T + 1, :]
    share_out(end)
    ddt_ref[...] = d_dt.T
    sum_ctx(end)
    sum_fsdp(end - 1)
    seam(end)
    last_rows = pltpu.make_async_copy(dx_ref.at[rest], dx_hbm.at[rest], load_sem.at[0])
    last_rows.start()

    def drain(c, _):
        if routed:
            chains[0][3](c)
            chains[1][3](c)
            return 0

        @pl.when(jnp.logical_not(last))
        def _():
            copy(c, out_f, in_f, send_f, recv_f, up).wait_send()

        @pl.when(jnp.logical_not(first))
        def _():
            copy(c, out_b, in_b, send_b, recv_b, down).wait_send()

        return 0

    lax.fori_loop(0, CHUNKS, drain, 0)
    if routed:
        chains[0][4]()
        chains[1][4]()

    @pl.when(jnp.logical_not(last))
    def _():
        for k in range(HALOS):
            halo(k).wait_send()

    def settle(g, _):
        for save in saves(g):
            save.wait()
        for r in range(1, count):
            scatter(g, lax.rem(me + r, count), me).wait_send()
        for r in range(1, depth):
            across(g, lax.rem(plane + r, depth), plane).wait_send()

        @pl.when(jnp.logical_not(first))
        def _():
            rim_copy(g).wait_send()

        return 0

    lax.fori_loop(0, GROUPS, settle, 0)
    sum_fsdp(end)
    for g in range(GROUPS):
        finish(g)
    last_rows.wait()
    dhead_ref[...] = total[end, GROUP_BLOCKS, 0:3, :]

    def settle_last(g, _):
        for r in range(1, count):
            gather(g, lax.rem(me + r, count), me).wait_send()
        return 0

    lax.fori_loop(0, GROUPS, settle_last, 0)


def land_kernel(*refs):
    n = (len(refs) - 2) // 3
    ins, outs, held = refs[:n], refs[n : 2 * n], refs[2 * n : 3 * n]
    in_sem, out_sem = refs[3 * n :]
    rows = T // LANDINGS
    parts = [(0, pl.ds(k * rows, rows)) for k in range(LANDINGS)]
    parts += [(k, pl.ds(0, ins[k].shape[0])) for k in range(1, n)]

    def arrive(s):
        k, r = parts[s]
        return pltpu.make_async_copy(ins[k].at[r], held[k].at[r], in_sem.at[s])

    def leave(s):
        k, r = parts[s]
        return pltpu.make_async_copy(held[k].at[r], outs[k].at[r], out_sem.at[s])

    for s in range(len(parts)):
        arrive(s).start()
    for s in range(len(parts)):
        arrive(s).wait()
        leave(s).start()
    for s in range(len(parts)):
        leave(s).wait()


def spots(count, far):
    return [pl.BlockSpec(memory_space=pl.ANY if k in far else pltpu.VMEM) for k in range(count)]


def call(kernel, out, scratch, args, limit, far_in, far_out, **params):
    return pl.pallas_call(
        kernel,
        out_shape=[jax.ShapeDtypeStruct(s, d) for s, d in out],
        in_specs=spots(len(args), far_in),
        out_specs=spots(len(out), far_out),
        scratch_shapes=scratch,
        compiler_params=pltpu.CompilerParams(vmem_limit_bytes=limit << 20, **params),
    )(*args)


def shards(xbc, dt_raw, dy, conv_params, head_params):
    count, depth = lax.axis_size("ctx"), lax.axis_size("fsdp")
    share = pl.cdiv(GROUP_BLOCKS + 1, count)
    wide, wide16 = pltpu.VMEM((T, X_WIDTH), F32), pltpu.VMEM((T, X_WIDTH), BF16)
    tall, tall16 = pltpu.VMEM((X_WIDTH, STATE), F32), pltpu.VMEM((X_WIDTH, STATE), BF16)
    small = pltpu.VMEM((T, LANES), F32)
    narrow = pltpu.VMEM((T, GROUPS * STATE), BF16)
    square = pltpu.VMEM((GROUPS, T, T), F32)
    edge = pltpu.VMEM((BLOCKS, RIM, LANES), F32)
    rim = pltpu.VMEM((GROUPS, GROUP_BLOCKS, RIM, LANES), F32)
    whole = pltpu.VMEM((GROUPS, share * count, 8, LANES), F32)
    dma = pltpu.SemaphoreType.DMA
    dx, ddt, dconv, dhead = call(
        functools.partial(main_kernel, (count, depth)),
        [((T, CHANNELS), BF16), ((HEADS, T), F32), ((CONV_W + 1, CHANNELS), F32), ((3, HEADS), F32)],
        [pltpu.VMEM((T, CHANNELS), BF16), wide16, pltpu.VMEM((T, CHANNELS), BF16),
         dma((3,)), dma((GROUPS, 3)),
         pltpu.VMEM((BLOCKS, 8 + T, LANES), F32), pltpu.VMEM((2, 16 + T, LANES), F32),
         pltpu.VMEM((T, CHANNELS), F32), wide16, wide, wide, tall, tall,
         tall16, tall16, tall16, tall16, wide, wide, wide,
         small, small, small, small, narrow, narrow,
         square, square, small, small, pltpu.VMEM((2 * T + 8, HEADS), F32),
         edge, edge, rim, rim, pltpu.VMEM((BLOCKS, TAIL, LANES), F32),
         whole, pltpu.VMEM((GROUPS, count, share, 8, LANES), F32),
         pltpu.VMEM((GROUPS, share, 8, LANES), F32),
         pltpu.VMEM((GROUPS, depth, share, 8, LANES), F32), whole]
        + [tall16, small, small]
        + [dma((CHUNKS,))] * 7 + [dma((3,))] + [dma((HALOS,))] * 2 + [dma((GROUPS,))] * 2
        + [dma((GROUPS, count))] * 2 + [dma((GROUPS, depth))] * 2 + [dma((GROUPS, count))] * 2,
        (xbc[0], dt_raw[0], dy[0], conv_params, head_params),
        far_in=(0, 2),
        far_out=(0,),
        limit=63,
        collective_id=0,
        has_side_effects=True,
    )
    results = (dx, ddt, dconv, dhead)
    anywhere = [pl.BlockSpec(memory_space=pl.ANY)] * len(results)
    dx, ddt, dconv, dhead = pl.pallas_call(
        land_kernel,
        out_shape=[jax.ShapeDtypeStruct(r.shape, r.dtype) for r in results],
        in_specs=anywhere,
        out_specs=anywhere,
        scratch_shapes=[pltpu.VMEM(r.shape, r.dtype) for r in results]
        + [dma((LANDINGS + len(results) - 1,))] * 2,
    )(*results)
    return dx[None], ddt[None], dconv, dhead


def solution(mesh):
    return jax.shard_map(
        shards,
        mesh=mesh,
        in_specs=(P("fsdp", "ctx", None), P("fsdp", None, "ctx"), P("fsdp", "ctx", None), P(), P()),
        out_specs=(P("fsdp", "ctx", None), P("fsdp", None, "ctx"), P(), P()),
        check_vma=False,
    )
```
